128 devices in a mesh: aux: 8 (over z_hi, y), vir: 16 (over z_lo, x, core).
Axes of the slice: x: 4, y: 4, z: 4 (z_hi: 2, z_lo: 2; z = z_hi * 2 + z_lo), core: 2. Of those that a mesh axis runs over, the one named last changes fastest.
Arguments:
- orbitals: bfloat16 [8192, 2, 4096], P('aux', None, 'vir'), may hold values from -0.5390625 to 0.5390625
- screened: bfloat16 [8192, 8192], P('vir', 'aux'), may hold values from -0.0625 to 0.0625
- density_in: float32 [4096, 4096], P('aux', 'vir'), may hold values from -6 to 6
Outputs:
- density: float32 [4096, 4096], P('aux', 'vir')
The draws below stay inside these ranges and needn't reach their ends.
All inputs are finite; a program needn't handle non-finite values.
Results may differ from the reference program's by a relative error of at most 0.008.
Values may be sent and summed in bfloat16 or wider, within the bound.
No kernel may reach another device: no remote copies, remote signals or barrier semaphores. Data moves between devices by JAX's collectives and lax.ppermute only.
A program may use at most 128 MiB of HBM per device.

```python
import jax
import jax.numpy as jnp
from jax import lax

V = 4096
NAUX = 8192
OCC = 2
AUX_DEV = 1024
N_AUX = 8


def levels(own_key, extent, shards, low, largest):
    def one(position, parts):
        heights = jax.random.uniform(jax.random.fold_in(jax.random.fold_in(own_key, 6), position), (parts,), jnp.float32, low / len(shards), largest / len(shards))
        return jnp.repeat(jnp.exp(heights), extent[position] // parts).reshape((-1,) + (1,) * (len(extent) - position - 1))

    loudness = one(*shards[0])
    for cut in shards[1:]:
        loudness = loudness * one(*cut)
    return loudness


def normal_values(key, extent, spread, limit, pieces=(), dtype=jnp.bfloat16):
    values = spread * jax.random.normal(key, extent, jnp.float32)
    if pieces:
        values = values * levels(key, extent, pieces, -0.22, 0.18)
    return jnp.clip(values, -limit, limit).astype(dtype)


def setup_inputs(seed: int = 0) -> dict:
    key_of = jax.random.split(jax.random.key(seed), 4)
    return {
        "orbitals": normal_values(key_of[0], (NAUX, OCC, V), 0.09, 0.5390625, ((0, 8), (2, 16))),
        "screened": normal_values(key_of[1], (NAUX, NAUX), NAUX ** -0.5, 0.0625, ((0, 16), (1, 8))),
        "density_in": normal_values(key_of[2], (V, V), 1.0, 6.0, ((0, 8), (1, 16)), jnp.float32),
    }


def reference(orbitals, screened, density_in):
    flat_orb = orbitals.reshape(NAUX, OCC * V)
    screened_orb = jnp.dot(screened.T, flat_orb, preferred_element_type=jnp.float32).astype(jnp.bfloat16)
    block_left = orbitals.reshape(N_AUX, AUX_DEV * OCC, V)
    block_right = screened_orb.reshape(N_AUX, AUX_DEV * OCC, V)

    def accumulate(running, pair):
        left_part, right_part = pair
        product = lax.dot_general(left_part, right_part, (((0,), (0,)), ((), ())), preferred_element_type=jnp.float32)
        rounded = lax.optimization_barrier(product.astype(jnp.bfloat16))
        return running + rounded.astype(jnp.float32), None

    summed, _ = lax.scan(accumulate, jnp.zeros((V, V), jnp.float32), (block_left, block_right))
    return density_in + summed
```

```python
import functools

import jax
import jax.numpy as jnp
from jax import lax
from jax.experimental import pallas as pl
from jax.experimental.pallas import tpu as pltpu
from jax.sharding import Mesh
from jax.sharding import PartitionSpec as P

AXES = ("zh", "y", "zl", "x", "c")
BF = jnp.bfloat16
F32 = jnp.float32
ANY = pl.BlockSpec(memory_space=pl.ANY)
VMEM = pl.BlockSpec(memory_space=pltpu.VMEM)
SMEM = pl.BlockSpec(memory_space=pltpu.SMEM)


def flat(x, y, z, c):
    x, y, z = x % 4, y % 4, z % 4
    return ((z // 2) * 4 + y) * 16 + (z % 2) * 8 + x * 2 + c


def table(move):
    pairs = []
    for x in range(4):
        for y in range(4):
            for z in range(4):
                for c in range(2):
                    pairs.append((flat(x, y, z, c), flat(*move(x, y, z, c))))
    return sorted(pairs)


def turn(c):
    return 1 - 2 * c


XF = table(lambda x, y, z, c: (x + turn(c), y, z, c))
XG = table(lambda x, y, z, c: (x - turn(c), y, z, c))
YF = table(lambda x, y, z, c: (x, y + turn(c), z, c))
YG = table(lambda x, y, z, c: (x, y - turn(c), z, c))
ZF = table(lambda x, y, z, c: (x, y, z + turn(c), c))
ZG = table(lambda x, y, z, c: (x, y, z - turn(c), c))
Z2 = table(lambda x, y, z, c: (x, y, z + 2, c))
ZN = table(lambda x, y, z, c: (x, y, z ^ 1, c))
CC = table(lambda x, y, z, c: (x, y, z, 1 - c))
ZNC = table(lambda x, y, z, c: (x, y, z ^ 1, 1 - c))


def send(v, pairs):
    return lax.ppermute(v, AXES, pairs)


def ring_gather(v, forward, backward):
    f = send(v, forward)
    g = send(v, backward)
    return v, f, g, send(f, forward)


def first_kernel(idx, w0, w1, w2, w3, b0, b1, b2, b3, t0, t1, t2, t3, wv, bv, wsem, bsem):
    ws, bs = (w0, w1, w2, w3), (b0, b1, b2, b3)
    for k in range(4):
        slot = idx[4 + k]
        pltpu.make_async_copy(bs[k], bv.at[slot], bsem.at[slot]).start()
    for k in range(4):
        slot = idx[k]
        pltpu.make_async_copy(ws[k], wv.at[slot], wsem.at[slot]).start()
    for k in range(4):
        pltpu.make_async_copy(bs[k], bv.at[k], bsem.at[k]).wait()
    outs = (t0, t1, t2, t3)
    half = wv.shape[2] // 2
    wide = bv.shape[3]
    for j in (2, 1, 3, 0):
        pltpu.make_async_copy(ws[j], wv.at[j], wsem.at[j]).wait()
        out = outs[j]

        def body(n, carry, j=j, out=out):
            i, low = n // 2, n % 2
            acc = jnp.dot(wv[j, :, :half], bv[low, i], preferred_element_type=F32)
            acc += jnp.dot(wv[j, :, half:], bv[2 + low, i], preferred_element_type=F32)
            out[:, pl.ds(pl.multiple_of(n * wide, wide), wide)] = acc.astype(BF)
            return carry

        lax.fori_loop(0, 4, body, 0)


def first_product(idx, ws, bs):
    rows, depth = ws[0].shape
    occ, depth_one, wide = bs[0].shape
    out = jax.ShapeDtypeStruct((rows, 2 * occ * wide), BF)
    return pl.pallas_call(
        first_kernel,
        out_shape=(out,) * 4,
        in_specs=[SMEM] + [ANY] * 8,
        out_specs=(VMEM,) * 4,
        scratch_shapes=[
            pltpu.VMEM((4, rows, depth), BF),
            pltpu.VMEM((4, occ, depth_one, wide), BF),
            pltpu.SemaphoreType.DMA((4,)),
            pltpu.SemaphoreType.DMA((4,)),
        ],
        compiler_params=pltpu.CompilerParams(vmem_limit_bytes=40 << 20),
        cost_estimate=pl.CostEstimate(
            flops=2 * 4 * rows * depth * 2 * occ * wide,
            bytes_accessed=4 * rows * depth * 2 + 4 * occ * depth_one * wide * 2 + 4 * rows * 4 * wide * 2,
            transcendentals=0,
        ),
        name="first_product",
    )(idx, *ws, *bs)


def split_kernel(idx, a, b, c, o0, o1, o2, o3):
    for k, out in enumerate((o0, o1, o2, o3)):
        for i in range(2):
            at = pl.ds(pl.multiple_of(i * 512 + idx[k] * 128, 128), 128)
            total = a[:, at].astype(F32) + b[:, at].astype(F32) + c[:, at].astype(F32)
            out[:, i * 128 : (i + 1) * 128] = total.astype(BF)


def split_sum(idx, a, b, c):
    out = jax.ShapeDtypeStruct((a.shape[0], 256), BF)
    return pl.pallas_call(
        split_kernel,
        out_shape=(out,) * 4,
        in_specs=[SMEM] + [VMEM] * 3,
        out_specs=(VMEM,) * 4,
        compiler_params=pltpu.CompilerParams(vmem_limit_bytes=8 << 20),
        cost_estimate=pl.CostEstimate(flops=3 * a.size, bytes_accessed=8 * a.size, transcendentals=0),
        name="split_sum",
    )(idx, a, b, c)


def second_kernel(idx, *refs):
    ts, bs, ds = refs[:8], refs[8:16], refs[16:20]
    tv, tt, bv, tsem, bsem = refs[20:]
    for k in range(8):
        slot = idx[8 + k]
        pltpu.make_async_copy(bs[k], bv.at[slot], bsem.at[slot]).start()
    for ch in range(2):
        for k in range(4):
            slot = idx[4 * ch + k]
            pltpu.make_async_copy(ts[4 * ch + k], tv.at[ch, slot], tsem.at[ch, slot]).start()
    for ch in range(2):
        for j in range(4):
            pltpu.make_async_copy(ts[4 * ch + j], tv.at[ch, j], tsem.at[ch, j]).wait()

            def body(rz, carry, ch=ch, j=j):
                for i in range(2):
                    at = pl.ds(pl.multiple_of(idx[16 + ch * 8 + rz * 2 + i] * 256, 256), 256)
                    tt[j * 128 : (j + 1) * 128, at] = tv[ch, j, rz, :, i * 128 : (i + 1) * 128].T
                return carry

            lax.fori_loop(0, 4, body, 0)
    for k in range(8):
        pltpu.make_async_copy(bs[k], bv.at[k], bsem.at[k]).wait()

    def column(n, carry):
        for m in range(2):
            acc = jnp.zeros((256, 256), F32)
            for high in range(2):
                for i in range(2):
                    at = (high * 2 + i) * 1024
                    acc += jnp.dot(
                        tt[m * 256 : (m + 1) * 256, at : at + 1024],
                        bv[high * 4 + n, i],
                        preferred_element_type=F32,
                    )
            at = pl.ds(pl.multiple_of(n * 256, 256), 256)
            ds[2 * m][:, at] = acc[:128].astype(BF)
            ds[2 * m + 1][:, at] = acc[128:].astype(BF)
        return carry

    lax.fori_loop(0, 4, column, 0)


def second_product(idx, ts, bs):
    out = jax.ShapeDtypeStruct((128, 1024), BF)
    return pl.pallas_call(
        second_kernel,
        out_shape=(out,) * 4,
        in_specs=[SMEM] + [ANY] * 16,
        out_specs=(VMEM,) * 4,
        scratch_shapes=[
            pltpu.VMEM((2, 4) + ts[0].shape, BF),
            pltpu.VMEM((512, 4096), BF),
            pltpu.VMEM((8,) + bs[0].shape, BF),
            pltpu.SemaphoreType.DMA((2, 4)),
            pltpu.SemaphoreType.DMA((8,)),
        ],
        compiler_params=pltpu.CompilerParams(vmem_limit_bytes=48 << 20),
        cost_estimate=pl.CostEstimate(
            flops=2 * 512 * 4096 * 1024, bytes_accessed=(8 + 4 + 1) << 20, transcendentals=0
        ),
        name="second_product",
    )(idx, *ts, *bs)


def tail_kernel(idx, a, b, c, o0, o1, o2, o3):
    for k, out in enumerate((o0, o1, o2, o3)):
        at = pl.ds(pl.multiple_of(idx[k] * 256, 256), 256)
        total = a[:, at].astype(F32) + b[:, at].astype(F32) + c[:, at].astype(F32)
        out[...] = total.astype(out.dtype)


def tail_split(idx, a, b, c):
    rows = a.shape[0]
    near = jax.ShapeDtypeStruct((rows, 256), BF)
    return pl.pallas_call(
        tail_kernel,
        out_shape=(jax.ShapeDtypeStruct((rows, 256), F32), near, near, near),
        in_specs=[SMEM] + [VMEM] * 3,
        out_specs=(VMEM,) * 4,
        compiler_params=pltpu.CompilerParams(vmem_limit_bytes=8 << 20),
        name="tail_split",
    )(idx, a, b, c)


def finish_kernel(idx, density, p0, p1, p2, p3, out):
    for k, piece in enumerate((p0, p1, p2, p3)):
        at = pl.ds(pl.multiple_of(idx[k] * 128, 128), 128)
        out[at, :] = density[at, :] + piece[...].astype(F32)


def finish(idx, density, pieces):
    return pl.pallas_call(
        finish_kernel,
        out_shape=jax.ShapeDtypeStruct(density.shape, F32),
        in_specs=[SMEM] + [VMEM] * 5,
        out_specs=VMEM,
        compiler_params=pltpu.CompilerParams(vmem_limit_bytes=8 << 20),
        name="finish",
    )(idx, density, *pieces)


def ints(values):
    return jnp.stack([jnp.asarray(v, jnp.int32) for v in values])


def shards(orbitals, screened, density_in):
    zh, y, zl, x, c = (lax.axis_index(name) for name in AXES)
    z = 2 * zh + zl
    s = 1 - 2 * c
    mod4 = lambda v: lax.rem(v + 8, 4)

    keep = lax.dynamic_slice_in_dim(screened, zh * 256, 256, 0)
    give = lax.dynamic_slice_in_dim(screened, (1 - zh) * 256, 256, 0)
    w = jnp.concatenate([keep, send(give, Z2)], axis=1)
    w_own, w_f, w_g, w_ff = ring_gather(w, XF, XG)
    w_mine = (w_own, w_g, w_ff, w_f)
    w_peer = (send(w_own, CC), send(w_f, CC), send(w_ff, CC), send(w_g, CC))

    b = jnp.transpose(orbitals, (1, 0, 2))
    b_own, b_f, b_g, b_ff = ring_gather(b, ZF, ZG)
    b_mine = (b_own, b_g, b_ff, b_f)
    b_peer = (send(b_own, CC), send(b_f, CC), send(b_ff, CC), send(b_g, CC))

    z_at = [mod4(z + s * k) for k in range(4)]
    j0 = s * (x - y)
    w_slot = [mod4(j0 + k) for k in range(4)]
    b_slot = [(v // 2 ^ zh) * 2 + v % 2 for v in z_at]
    first_idx = ints(w_slot + b_slot)
    split_idx = ints([z, mod4(z + s), mod4(z - s), mod4(z + 2)])

    chunks = []
    for ws in (w_mine, w_peer):
        t0, t1, t2, t3 = first_product(first_idx, ws, b_mine)
        r1 = send(t2, YF)
        mid = (t1.astype(F32) + r1.astype(F32)).astype(BF)
        t_own, t_f, t_g, t_2 = split_sum(split_idx, t0, send(mid, YF), send(t3, YG))
        t = jnp.stack([t_own, send(t_f, ZF), send(t_g, ZG), send(t_2, Z2)])
        own, f, g, ff = ring_gather(t, XF, XG)
        chunks.append((own, g, ff, f))

    from_z = [z, mod4(z - s), mod4(z + s), mod4(z + 2)]
    places = []
    for core in (c, 1 - c):
        for v in from_z:
            for i in range(2):
                places.append((((v % 2) * 2 + i) * 2 + core) * 2 + v // 2)
    b2_slot = [(v // 2) * 4 + (v % 2) * 2 + core for core in (c, 1 - c) for v in z_at]
    second_idx = ints(w_slot + w_slot + b2_slot + places)
    d0, d1, d2, d3 = second_product(second_idx, chunks[0] + chunks[1], b_mine + b_peer)

    r1 = send(d2, YF)
    mid = (d1.astype(F32) + r1.astype(F32)).astype(BF)
    tail_idx = ints([zl * 2 + c, (1 - zl) * 2 + c, zl * 2 + 1 - c, (1 - zl) * 2 + 1 - c])
    p_own, p_n, p_c, p_nc = tail_split(tail_idx, d0, send(mid, YF), send(d3, YG))
    finish_idx = ints([c * 2 + zl, c * 2 + 1 - zl, (1 - c) * 2 + zl, (1 - c) * 2 + 1 - zl])
    return finish(finish_idx, density_in, (p_own, send(p_n, ZN), send(p_c, CC), send(p_nc, ZNC)))


def solution(mesh):
    fine = Mesh(mesh.devices.reshape(2, 4, 2, 4, 2), AXES)
    row, col = ("zh", "y"), ("zl", "x", "c")
    return jax.shard_map(
        shards,
        mesh=fine,
        in_specs=(P(row, None, col), P(col, row), P(row, col)),
        out_specs=P(row, col),
        check_vma=False,
    )
```

```python
import functools

import jax
import jax.numpy as jnp
from jax import lax
from jax.experimental import pallas as pl
from jax.experimental.pallas import tpu as pltpu
from jax.sharding import Mesh
from jax.sharding import PartitionSpec as P


AXES = ("zh", "y", "zl", "x", "c")
BF = jnp.bfloat16
F32 = jnp.float32
ANY = pl.BlockSpec(memory_space=pl.ANY)
HBM = pl.BlockSpec(memory_space=pltpu.HBM)
VMEM = pl.BlockSpec(memory_space=pltpu.VMEM)
SMEM = pl.BlockSpec(memory_space=pltpu.SMEM)


def flat(x, y, z, c):
    x, y, z = x % 4, y % 4, z % 4
    return ((z // 2) * 4 + y) * 16 + (z % 2) * 8 + x * 2 + c


def table(move):
    pairs = []
    for x in range(4):
        for y in range(4):
            for z in range(4):
                for c in range(2):
                    pairs.append((flat(x, y, z, c), flat(*move(x, y, z, c))))
    return sorted(pairs)


def turn(c):
    return 1 - 2 * c


XF = table(lambda x, y, z, c: (x + turn(c), y, z, c))
XG = table(lambda x, y, z, c: (x - turn(c), y, z, c))
YF = table(lambda x, y, z, c: (x, y + turn(c), z, c))
YG = table(lambda x, y, z, c: (x, y - turn(c), z, c))
ZF = table(lambda x, y, z, c: (x, y, z + turn(c), c))
ZG = table(lambda x, y, z, c: (x, y, z - turn(c), c))
Z2 = table(lambda x, y, z, c: (x, y, z + 2, c))
ZN = table(lambda x, y, z, c: (x, y, z ^ 1, c))
CC = table(lambda x, y, z, c: (x, y, z, 1 - c))
ZNC = table(lambda x, y, z, c: (x, y, z ^ 1, 1 - c))


def send(v, pairs):
    return lax.ppermute(v, AXES, pairs)


def call(kernel, outs, out_specs, in_specs, scratch, flops=0, aliases=None, limit=16):
    return pl.pallas_call(
        kernel,
        out_shape=outs,
        in_specs=in_specs,
        out_specs=out_specs,
        scratch_shapes=scratch,
        input_output_aliases=aliases or {},
        compiler_params=pltpu.CompilerParams(vmem_limit_bytes=limit << 20),
        cost_estimate=pl.CostEstimate(flops=flops, bytes_accessed=4 << 20, transcendentals=0),
    )


def sems(*shape):
    return pltpu.SemaphoreType.DMA(shape)


def run_copies(copies):
    for copy in copies:
        copy.start()
    return copies


def finish_copies(copies):
    for copy in copies:
        copy.wait()


def first_kernel(slots, idx, *refs):
    n = len(slots)
    ws, bs, outs, (wv, bv, ov, wsem, bsem, osem) = refs[:16], refs[16:20], refs[20 : 20 + n], refs[20 + n :]

    def w_copy(at, q, k):
        place = wv.at[at, pl.ds(q // 2 * 256, 256), pl.ds(q % 2 * 1024, 1024)]
        return pltpu.make_async_copy(ws[q * 4 + k], place, wsem.at[at, q])

    def b_place(v):
        return bv.at[v % 2, pl.ds(pl.multiple_of(v // 2 * 1024, 1024), 1024)]

    b_copies = run_copies([pltpu.make_async_copy(bs[k], b_place(idx[4 + k]), bsem.at[k]) for k in range(4)])
    for at, j in enumerate(slots):
        for k in range(4):

            @pl.when(idx[j] == k)
            def _(at=at, k=k):
                run_copies([w_copy(at, q, k) for q in range(4)])

    finish_copies(b_copies)
    writes = []
    for at in range(n):
        finish_copies([w_copy(at, q, 0) for q in range(4)])
        for low in range(2):
            acc = jnp.dot(wv[at], bv[low], preferred_element_type=F32)
            ov[at, :, low * 256 : (low + 1) * 256] = acc.astype(BF)
        writes += run_copies([pltpu.make_async_copy(ov.at[at], outs[at], osem.at[at])])
    finish_copies(writes)


def first_product(slots, idx, ws, bs):
    n = len(slots)
    scratch = [
        pltpu.VMEM((n, 512, 2048), BF),
        pltpu.VMEM((2, 2048, 256), BF),
        pltpu.VMEM((n, 512, 512), BF),
        sems(n, 4),
        sems(4),
        sems(n),
    ]
    return call(
        functools.partial(first_kernel, slots),
        ((pltpu.HBM if n == 4 else jax.ShapeDtypeStruct)((512, 512), BF),) * n,
        (HBM if n == 4 else ANY,) * n,
        [SMEM] + [ANY] * 20,
        scratch,
        flops=n * 2 * 512 * 2048 * 512,
        limit=3 + (5 * n + 1) // 2,
    )(idx, *ws, *bs)


def split_kernel(idx, a, b, c, o0, o1, o2, o3):
    for k, out in enumerate((o0, o1, o2, o3)):
        at = pl.ds(pl.multiple_of(idx[k] * 128, 128), 128)
        total = a[:, at].astype(F32) + b[:, at].astype(F32) + c[:, at].astype(F32)
        out[...] = total.astype(BF)


def split_sum(idx, a, b, c):
    out = jax.ShapeDtypeStruct((a.shape[0], 128), BF)
    return pl.pallas_call(
        split_kernel,
        out_shape=(out,) * 4,
        in_specs=[SMEM] + [VMEM] * 3,
        out_specs=(VMEM,) * 4,
        compiler_params=pltpu.CompilerParams(vmem_limit_bytes=8 << 20),
        cost_estimate=pl.CostEstimate(flops=3 * a.size, bytes_accessed=8 * a.size, transcendentals=0),
        name="split_sum",
    )(idx, a, b, c)


def load_b_kernel(idx, *refs):
    bs, bv, sem = refs[:16], refs[16], refs[17]
    copies = []
    for i in range(2):
        for k in range(8):
            v = idx[k]
            at = pl.ds(pl.multiple_of(i * 2048 + v // 4 * 1024, 1024), 1024)
            copies.append(pltpu.make_async_copy(bs[i * 8 + k], bv.at[v % 4, at], sem.at[i * 8 + k]))
    finish_copies(run_copies(copies))


def load_b(idx, bs):
    return call(
        load_b_kernel, jax.ShapeDtypeStruct((4, 4096, 256), BF), VMEM, [SMEM] + [ANY] * 16, [sems(16)], limit=1
    )(idx, *bs)


def second_kernel(n_ts, idx, bv, *refs):
    ts, refs = refs[: 2 * n_ts], refs[2 * n_ts :]
    if n_ts == 1:
        early, outs, (tv, tt, every, tsem, esem, osem) = refs[0], refs[1:5], refs[5:]
        moves = run_copies(
            [
                pltpu.make_async_copy(early.at[pl.ds(n * 128, 128)], every.at[k], esem.at[n])
                for n, k in enumerate((0, 1, 3))
            ]
        )
    else:
        out, (tv, tt, tsem) = refs[0], refs[1:]
    copies = run_copies([pltpu.make_async_copy(t, tv.at[n], tsem.at[n]) for n, t in enumerate(ts)])
    for n, copy in enumerate(copies):
        copy.wait()
        k, i = n // 2, n % 2
        for rz in range(4):
            for ch in range(2):
                at = pl.ds(pl.multiple_of(i * 2048 + idx[8 + rz * 2 + ch] * 256, 256), 256)
                tt[k * 128 : (k + 1) * 128, at] = tv[n, rz, ch * 256 : (ch + 1) * 256, :].T
    for n in range(4):
        at = slice(n * 256, (n + 1) * 256)
        acc = jnp.dot(tt[...], bv[n], preferred_element_type=F32).astype(BF)
        if n_ts == 1:
            every[2, :, at] = acc
        else:
            out[:, at] = acc
    if n_ts == 1:
        finish_copies(moves)
        finish_copies(
            run_copies([pltpu.make_async_copy(every.at[idx[16 + j]], outs[j], osem.at[j]) for j in range(4)])
        )


def second_product(idx, bv, ts, early=None):
    n = len(ts) // 2
    scratch = [pltpu.VMEM((2 * n, 4, 512, 128), BF), pltpu.VMEM((n * 128, 4096), BF)]
    if early is None:
        outs, specs, more = jax.ShapeDtypeStruct((n * 128, 1024), BF), VMEM, ()
        scratch += [sems(2 * n)]
    else:
        outs, specs, more = (jax.ShapeDtypeStruct((128, 1024), BF),) * 4, (ANY,) * 4, (early,)
        scratch += [pltpu.VMEM((4, 128, 1024), BF), sems(2), sems(3), sems(4)]
    return call(
        functools.partial(second_kernel, n),
        outs,
        specs,
        [SMEM, VMEM] + [ANY] * (2 * n + len(more)),
        scratch,
        flops=2 * n * 128 * 4096 * 1024,
        limit=12,
    )(idx, bv, *ts, *more)


def tail_kernel(idx, a, b, c, o0, o1, o2, o3):
    for k, out in enumerate((o0, o1, o2, o3)):
        at = pl.ds(pl.multiple_of(idx[k] * 256, 256), 256)
        total = a[:, at].astype(F32) + b[:, at].astype(F32) + c[:, at].astype(F32)
        out[...] = total.astype(out.dtype)


def tail_split(idx, a, b, c):
    rows = a.shape[0]
    near = jax.ShapeDtypeStruct((rows, 256), BF)
    return pl.pallas_call(
        tail_kernel,
        out_shape=(jax.ShapeDtypeStruct((rows, 256), F32), near, near, near),
        in_specs=[SMEM] + [VMEM] * 3,
        out_specs=(VMEM,) * 4,
        compiler_params=pltpu.CompilerParams(vmem_limit_bytes=8 << 20),
        name="tail_split",
    )(idx, a, b, c)


def finish_kernel(idx, density, p0, p1, p2, p3, out):
    for k, piece in enumerate((p0, p1, p2, p3)):
        at = pl.ds(pl.multiple_of(idx[k] * 128, 128), 128)
        out[at, :] = density[at, :] + piece[...].astype(F32)


def finish(idx, density, pieces):
    return pl.pallas_call(
        finish_kernel,
        out_shape=jax.ShapeDtypeStruct(density.shape, F32),
        in_specs=[SMEM] + [VMEM] * 5,
        out_specs=VMEM,
        compiler_params=pltpu.CompilerParams(vmem_limit_bytes=8 << 20),
        name="finish",
    )(idx, density, *pieces)


def ints(values):
    return jnp.stack([jnp.asarray(v, jnp.int32) for v in values])


def step(orbitals, screened, density_in):
    zh, y, zl, x, c = (lax.axis_index(name) for name in AXES)
    z = 2 * zh + zl
    s = 1 - 2 * c
    mod4 = lambda v: lax.rem(v + 8, 4)
    z_at = [mod4(z + s * k) for k in range(4)]
    piece = [mod4(j - s * (x - y)) for j in range(4)]
    first_idx = ints(piece + [(v // 2 ^ zh) * 2 + v % 2 for v in z_at])
    split_idx = ints([z, mod4(z + s), mod4(z - s), mod4(z + 2)])
    from_z = [z, mod4(z - s), mod4(z + s), mod4(z + 2)]
    places = [((v % 2) * 2 + core) * 2 + v // 2 for v in from_z for core in (c, 1 - c)]
    b2_slot = [(v // 2) * 4 + (v % 2) * 2 + core for core in (c, 1 - c) for v in z_at]
    second_idx = ints(b2_slot + places + piece)
    tail_idx = ints([zl * 2 + c, (1 - zl) * 2 + c, zl * 2 + 1 - c, (1 - zl) * 2 + 1 - c])
    finish_idx = ints([c * 2 + zl, c * 2 + 1 - zl, (1 - c) * 2 + zl, (1 - c) * 2 + 1 - zl])

    keep = lax.dynamic_slice_in_dim(screened, zh * 256, 256, 0)
    give = lax.dynamic_slice_in_dim(screened, (1 - zh) * 256, 256, 0)
    b = jnp.transpose(orbitals, (1, 0, 2))
    b0, b1 = b[0], b[1]
    other = send(give, Z2)
    wa_f = send(keep, XF)
    wa_g = send(keep, XG)
    b0_f = send(b0, ZF)
    b0_g = send(b0, ZG)
    wa_ff = send(wa_f, XF)
    wb_f = send(other, XF)
    wb_g = send(other, XG)
    b0_ff = send(b0_f, ZF)
    b1_f = send(b1, ZF)
    b1_g = send(b1, ZG)
    wb_ff = send(wb_g, XG)
    b1_ff = send(b1_g, ZG)
    wa = (keep, wa_g, wa_ff, wa_f)
    wb = (other, wb_g, wb_ff, wb_f)
    swap = lambda four: tuple(send(four[k], CC) for k in (0, 3, 2, 1))
    ws = wa + wb + swap(wa) + swap(wb)
    bs = ((b0, b0_g, b0_ff, b0_f), (b1, b1_g, b1_ff, b1_f))

    t2, t1, t3, t0 = [None] * 2, [None] * 2, [None] * 2, [None] * 2
    (t2[0],) = first_product((2,), first_idx, ws, bs[0])
    t1[0], t3[0], t0[0] = first_product((1, 3, 0), first_idx, ws, bs[0])
    t2[1], t1[1], t3[1], t0[1] = first_product((2, 1, 3, 0), first_idx, ws, bs[1])
    gathered = []
    for i in range(2):
        r1 = send(t2[i], YF)
        mid = (t1[i].astype(F32) + r1.astype(F32)).astype(BF)
        r_g = send(t3[i], YG)
        r_f = send(mid, YF)
        t_own, t_f, t_g, t_2 = split_sum(split_idx, t0[i], r_f, r_g)
        t_2 = send(t_2, Z2)
        t_f = send(t_f, ZF)
        t_g = send(t_g, ZG)
        t = jnp.stack([t_own, t_f, t_g, t_2])
        f = send(t, XF)
        g = send(t, XG)
        far = send(f, XF) if i == 0 else send(g, XG)
        gathered.append((t, g, far, f))
    b_all = load_b(second_idx, [v for i in range(2) for v in bs[i] + swap(bs[i])])
    early = second_product(second_idx, b_all, [gathered[i][k] for k in (0, 1, 3) for i in range(2)])
    d0, d1, d2, d3 = second_product(second_idx, b_all, [gathered[i][2] for i in range(2)], early)

    r1 = send(d2, YF)
    r_g = send(d3, YG)
    mid = (d1.astype(F32) + r1.astype(F32)).astype(BF)
    p_own, p_n, p_c, p_nc = tail_split(tail_idx, d0, send(mid, YF), r_g)
    p_nc = send(p_nc, ZNC)
    p_n = send(p_n, ZN)
    p_c = send(p_c, CC)
    return finish(finish_idx, density_in, (p_own, p_n, p_c, p_nc))


def solution(mesh):
    fine = Mesh(mesh.devices.reshape(2, 4, 2, 4, 2), AXES)
    row, col = ("zh", "y"), ("zl", "x", "c")
    return jax.shard_map(
        step,
        mesh=fine,
        in_specs=(P(row, None, col), P(col, row), P(row, col)),
        out_specs=P(row, col),
        check_vma=False,
    )
```

```python
import functools

import jax
import jax.numpy as jnp
from jax import lax
from jax.experimental import pallas as pl
from jax.experimental.pallas import tpu as pltpu
from jax.sharding import Mesh
from jax.sharding import PartitionSpec as P


AXES = ("zh", "y", "zl", "x", "c")
BF = jnp.bfloat16
F32 = jnp.float32
ANY = pl.BlockSpec(memory_space=pl.ANY)
VMEM = pl.BlockSpec(memory_space=pltpu.VMEM)
SMEM = pl.BlockSpec(memory_space=pltpu.SMEM)
HBM = pl.BlockSpec(memory_space=pltpu.HBM)
CHUNKS = (((0, 0), (1, 0)), ((0, 1),), ((1, 1),))


def flat(x, y, z, c):
    x, y, z = x % 4, y % 4, z % 4
    return ((z // 2) * 4 + y) * 16 + (z % 2) * 8 + x * 2 + c


def table(move):
    pairs = []
    for x in range(4):
        for y in range(4):
            for z in range(4):
                for c in range(2):
                    pairs.append((flat(x, y, z, c), flat(*move(x, y, z, c))))
    return sorted(pairs)


def turn(c):
    return 1 - 2 * c


XF = table(lambda x, y, z, c: (x + turn(c), y, z, c))
XG = table(lambda x, y, z, c: (x - turn(c), y, z, c))
YF = table(lambda x, y, z, c: (x, y + turn(c), z, c))
YG = table(lambda x, y, z, c: (x, y - turn(c), z, c))
ZF = table(lambda x, y, z, c: (x, y, z + turn(c), c))
ZG = table(lambda x, y, z, c: (x, y, z - turn(c), c))
Y2 = table(lambda x, y, z, c: (x, y + 2, z, c))
Z2 = table(lambda x, y, z, c: (x, y, z + 2, c))
ZN = table(lambda x, y, z, c: (x, y, z ^ 1, c))
CC = table(lambda x, y, z, c: (x, y, z, 1 - c))
ZNC = table(lambda x, y, z, c: (x, y, z ^ 1, 1 - c))


def send(v, pairs):
    return lax.ppermute(v, AXES, pairs)


def call(kernel, outs, out_specs, in_specs, scratch, flops=0, aliases=None, limit=16):
    return pl.pallas_call(
        kernel,
        out_shape=outs,
        in_specs=in_specs,
        out_specs=out_specs,
        scratch_shapes=scratch,
        input_output_aliases=aliases or {},
        compiler_params=pltpu.CompilerParams(vmem_limit_bytes=limit << 20),
        cost_estimate=pl.CostEstimate(flops=flops, bytes_accessed=4 << 20, transcendentals=0),
    )


def sems(*shape):
    return pltpu.SemaphoreType.DMA(shape)


def run_copies(copies):
    for copy in copies:
        copy.start()
    return copies


def finish_copies(copies):
    for copy in copies:
        copy.wait()


def first_kernel(slots, idx, *refs):
    n = len(slots)
    ws, bs, outs, (wv, bv, ov, wsem, bsem, osem) = refs[:16], refs[16:20], refs[20 : 20 + n], refs[20 + n :]

    def w_copy(at, q, k):
        place = wv.at[at, pl.ds(q // 2 * 256, 256), pl.ds(q % 2 * 1024, 1024)]
        return pltpu.make_async_copy(ws[q * 4 + k], place, wsem.at[at, q])

    def b_place(v):
        return bv.at[v % 2, pl.ds(pl.multiple_of(v // 2 * 1024, 1024), 1024)]

    b_copies = run_copies([pltpu.make_async_copy(bs[k], b_place(idx[4 + k]), bsem.at[k]) for k in range(4)])
    for at, j in enumerate(slots):
        for k in range(4):

            @pl.when(idx[j] == k)
            def _(at=at, k=k):
                run_copies([w_copy(at, q, k) for q in range(4)])

    finish_copies(b_copies)
    writes = []
    for at in range(n):
        finish_copies([w_copy(at, q, 0) for q in range(4)])
        for low in range(2):
            acc = jnp.dot(wv[at], bv[low], preferred_element_type=F32)
            ov[at, :, low * 256 : (low + 1) * 256] = acc.astype(BF)
        writes += run_copies([pltpu.make_async_copy(ov.at[at], outs[at], osem.at[at])])
    finish_copies(writes)


def first_product(slots, idx, ws, bs):
    n = len(slots)
    scratch = [
        pltpu.VMEM((n, 512, 2048), BF),
        pltpu.VMEM((2, 2048, 256), BF),
        pltpu.VMEM((n, 512, 512), BF),
        sems(n, 4),
        sems(4),
        sems(n),
    ]
    return call(
        functools.partial(first_kernel, slots),
        ((pltpu.HBM if n == 4 else jax.ShapeDtypeStruct)((512, 512), BF),) * n,
        (HBM if n == 4 else ANY,) * n,
        [SMEM] + [ANY] * 20,
        scratch,
        flops=n * 2 * 512 * 2048 * 512,
        limit=3 + (5 * n + 1) // 2,
    )(idx, *ws, *bs)


def split_kernel(idx, a, b, c, o0, o1, o2, o3):
    for k, out in enumerate((o0, o1, o2, o3)):
        at = pl.ds(pl.multiple_of(idx[k] * 128, 128), 128)
        total = a[:, at].astype(F32) + b[:, at].astype(F32) + c[:, at].astype(F32)
        out[...] = total.astype(BF)


def split_sum(idx, a, b, c):
    out = jax.ShapeDtypeStruct((a.shape[0], 128), BF)
    return pl.pallas_call(
        split_kernel,
        out_shape=(out,) * 4,
        in_specs=[SMEM] + [VMEM] * 3,
        out_specs=(VMEM,) * 4,
        compiler_params=pltpu.CompilerParams(vmem_limit_bytes=8 << 20),
        cost_estimate=pl.CostEstimate(flops=3 * a.size, bytes_accessed=8 * a.size, transcendentals=0),
        name="split_sum",
    )(idx, a, b, c)


def load_b_kernel(idx, *refs):
    bs, bv, sem = refs[:16], refs[16], refs[17]
    copies = []
    for i in range(2):
        for k in range(8):
            v = idx[k]
            at = pl.ds(pl.multiple_of(i * 2048 + v // 4 * 1024, 1024), 1024)
            copies.append(pltpu.make_async_copy(bs[i * 8 + k], bv.at[v % 4, at], sem.at[i * 8 + k]))
    finish_copies(run_copies(copies))


def load_b(idx, bs):
    return call(
        load_b_kernel,
        jax.ShapeDtypeStruct((4, 4096, 256), BF),
        VMEM,
        [SMEM] + [ANY] * 16,
        [sems(16)],
        limit=1,
    )(idx, *bs)


def second_kernel(ks, idx, bv, *refs):
    n_ts = len(ks) * len(CHUNKS)
    ts, refs = refs[:n_ts], refs[n_ts:]
    last = ks == (2,)
    if last:
        others, outs, refs = refs[:3], refs[3:7], refs[7:]
        every, esem, osem = refs[:3]
        refs = refs[3:]
        moves = run_copies(
            [
                pltpu.make_async_copy(other, every.at[k], esem.at[n])
                for n, (other, k) in enumerate(zip(others, (0, 1, 3)))
            ]
        )
    else:
        out, refs = refs[0], refs[1:]
    tt, tsem, tvs = refs[0], refs[1], refs[2:]
    copies = []
    for q, blocks in enumerate(CHUNKS):
        for n in range(len(ks)):
            m = q * len(ks) + n
            copies.append((q, n, pltpu.make_async_copy(ts[m], tvs[q].at[n], tsem.at[m])))
    run_copies([copy for _, _, copy in copies])
    for q, n, copy in copies:
        copy.wait()
        for rz in range(4):
            for r, (ch, i) in enumerate(CHUNKS[q]):
                at = pl.ds(pl.multiple_of(i * 2048 + idx[8 + rz * 2 + ch] * 256, 256), 256)
                tt[n * 128 : (n + 1) * 128, at] = tvs[q][n, rz, r * 256 : (r + 1) * 256, :].T
    for n in range(4):
        at = slice(n * 256, (n + 1) * 256)
        acc = jnp.dot(tt[...], bv[n], preferred_element_type=F32).astype(BF)
        if last:
            every[2, :, at] = acc
        else:
            out[:, at] = acc
    if last:
        finish_copies(moves)
        finish_copies(
            run_copies([pltpu.make_async_copy(every.at[idx[16 + j]], outs[j], osem.at[j]) for j in range(4)])
        )


def second_product(ks, idx, bv, ts, *early):
    n = len(ks)
    scratch = [pltpu.VMEM((n * 128, 4096), BF), sems(n * len(CHUNKS))]
    scratch += [pltpu.VMEM((n, 4, 256 * len(blocks), 128), BF) for blocks in CHUNKS]
    if early:
        outs, specs = (jax.ShapeDtypeStruct((128, 1024), BF),) * 4, (ANY,) * 4
        scratch = [pltpu.VMEM((4, 128, 1024), BF), sems(3), sems(4)] + scratch
    else:
        outs, specs = jax.ShapeDtypeStruct((n * 128, 1024), BF), VMEM
    return call(
        functools.partial(second_kernel, ks),
        outs,
        specs,
        [SMEM, VMEM] + [ANY] * (n * len(CHUNKS) + len(early)),
        scratch,
        flops=2 * n * 128 * 4096 * 1024,
        limit=12,
    )(idx, bv, *ts, *early)


def tail_kernel(idx, a, b, c, d, o0, o1, o2, o3):
    for k, out in enumerate((o0, o1, o2, o3)):
        at = pl.ds(pl.multiple_of(idx[k] * 256, 256), 256)
        total = a[:, at].astype(F32) + b[:, at].astype(F32)
        total += c[:, at].astype(F32) + d[:, at].astype(F32)
        out[...] = total.astype(out.dtype)


def tail_split(idx, a, b, c, d):
    rows = a.shape[0]
    near = jax.ShapeDtypeStruct((rows, 256), BF)
    return pl.pallas_call(
        tail_kernel,
        out_shape=(jax.ShapeDtypeStruct((rows, 256), F32), near, near, near),
        in_specs=[SMEM] + [VMEM] * 4,
        out_specs=(VMEM,) * 4,
        compiler_params=pltpu.CompilerParams(vmem_limit_bytes=8 << 20),
        name="tail_split",
    )(idx, a, b, c, d)


def finish_kernel(idx, density, p0, p1, p2, p3, out):
    for k, piece in enumerate((p0, p1, p2, p3)):
        at = pl.ds(pl.multiple_of(idx[k] * 128, 128), 128)
        out[at, :] = density[at, :] + piece[...].astype(F32)


def finish(idx, density, pieces):
    return pl.pallas_call(
        finish_kernel,
        out_shape=jax.ShapeDtypeStruct(density.shape, F32),
        in_specs=[SMEM] + [VMEM] * 5,
        out_specs=VMEM,
        compiler_params=pltpu.CompilerParams(vmem_limit_bytes=8 << 20),
        name="finish",
    )(idx, density, *pieces)


def ints(values):
    return jnp.stack([jnp.asarray(v, jnp.int32) for v in values])


def step(orbitals, screened, density_in):
    zh, y, zl, x, c = (lax.axis_index(name) for name in AXES)
    z = 2 * zh + zl
    s = 1 - 2 * c
    mod4 = lambda v: lax.rem(v + 8, 4)
    z_at = [mod4(z + s * k) for k in range(4)]
    piece = [mod4(j - s * (x - y)) for j in range(4)]
    first_idx = ints(piece + [(v // 2 ^ zh) * 2 + v % 2 for v in z_at])
    split_idx = ints([z, mod4(z + s), mod4(z - s), mod4(z + 2)])
    from_z = [z, mod4(z - s), mod4(z + s), mod4(z + 2)]
    places = [((v % 2) * 2 + core) * 2 + v // 2 for v in from_z for core in (c, 1 - c)]
    b2_slot = [(v // 2) * 4 + (v % 2) * 2 + core for core in (c, 1 - c) for v in z_at]
    second_idx = ints(b2_slot + places + piece)
    tail_idx = ints([zl * 2 + c, (1 - zl) * 2 + c, zl * 2 + 1 - c, (1 - zl) * 2 + 1 - c])
    finish_idx = ints([c * 2 + zl, c * 2 + 1 - zl, (1 - c) * 2 + zl, (1 - c) * 2 + 1 - zl])

    keep = lax.dynamic_slice_in_dim(screened, zh * 256, 256, 0)
    give = lax.dynamic_slice_in_dim(screened, (1 - zh) * 256, 256, 0)
    b = jnp.transpose(orbitals, (1, 0, 2))
    b0, b1 = b[0], b[1]
    other = send(give, Z2)
    wa_f = send(keep, XF)
    wa_g = send(keep, XG)
    b0_f = send(b0, ZF)
    b0_g = send(b0, ZG)
    wa_ff = send(wa_g, XG)
    wb_f = send(other, XF)
    wb_g = send(other, XG)
    b0_ff = send(b0_g, ZG)
    b1_f = send(b1, ZF)
    b1_g = send(b1, ZG)
    wb_ff = send(wb_f, XF)
    b1_ff = send(b1_f, ZF)
    wa = (keep, wa_g, wa_ff, wa_f)
    wb = (other, wb_g, wb_ff, wb_f)
    swap = lambda four: tuple(send(four[k], CC) for k in (0, 3, 2, 1))
    ws = wa + wb + swap(wa) + swap(wb)
    bs = ((b0, b0_g, b0_ff, b0_f), (b1, b1_g, b1_ff, b1_f))

    t2, t1, t3, t0 = [None] * 2, [None] * 2, [None] * 2, [None] * 2
    (t2[0],) = first_product((2,), first_idx, ws, bs[0])
    t1[0], t3[0], t0[0] = first_product((1, 3, 0), first_idx, ws, bs[0])
    t2[1], t1[1], t3[1], t0[1] = first_product((2, 1, 3, 0), first_idx, ws, bs[1])
    gathered = []
    for i in range(2):
        r1 = send(t2[i], YF)
        mid = (t1[i].astype(F32) + r1.astype(F32)).astype(BF)
        r_g = send(t3[i], YG)
        r_f = send(mid, YF)
        t_own, t_f, t_g, t_2 = split_sum(split_idx, t0[i], r_f, r_g)
        t_2 = send(t_2, Z2)
        t_f = send(t_f, ZF)
        t_g = send(t_g, ZG)
        four = [t_own, t_f, t_g, t_2]
        halves = [four] if i == 0 else [[t[:256] for t in four], [t[256:] for t in four]]
        for t in halves:
            n = len(gathered)
            t = jnp.stack(t)
            f = send(t, XF)
            g = send(t, XG)
            far = send(g, XG) if n else send(f, XF)
            gathered.append((t, g, far, f))
    b_all = load_b(second_idx, [v for i in range(2) for v in bs[i] + swap(bs[i])])

    def second(ks, *more):
        return second_product(ks, second_idx, b_all, [t[k] for t in gathered for k in ks], *more)

    others = second((0,)), second((1,)), second((3,))
    d0, d1, d2, d3 = second((2,), *others)

    d2, d1, d3 = send(d2, Y2), send(d1, YF), send(d3, YG)
    p_own, p_n, p_c, p_nc = tail_split(tail_idx, d0, d1, d3, d2)
    p_nc = send(p_nc, ZNC)
    p_n = send(p_n, ZN)
    p_c = send(p_c, CC)
    return finish(finish_idx, density_in, (p_own, p_n, p_c, p_nc))


def solution(mesh):
    fine = Mesh(mesh.devices.reshape(2, 4, 2, 4, 2), AXES)
    row, col = ("zh", "y"), ("zl", "x", "c")
    return jax.shard_map(
        step,
        mesh=fine,
        in_specs=(P(row, None, col), P(col, row), P(row, col)),
        out_specs=P(row, col),
        check_vma=False,
    )
```

```python
import functools

import jax
import jax.numpy as jnp
from jax import lax
from jax.experimental import pallas as pl
from jax.experimental.pallas import tpu as pltpu
from jax.sharding import Mesh
from jax.sharding import PartitionSpec as P


AXES = ("zh", "y", "zl", "x", "c")
BF = jnp.bfloat16
F32 = jnp.float32
ANY = pl.BlockSpec(memory_space=pl.ANY)
VMEM = pl.BlockSpec(memory_space=pltpu.VMEM)
SMEM = pl.BlockSpec(memory_space=pltpu.SMEM)
HBM = pl.BlockSpec(memory_space=pltpu.HBM)
CHUNKS = (((0, 0), (1, 0)), ((0, 1),), ((1, 1),))


def flat(x, y, z, c):
    x, y, z = x % 4, y % 4, z % 4
    return ((z // 2) * 4 + y) * 16 + (z % 2) * 8 + x * 2 + c


def table(move):
    pairs = []
    for x in range(4):
        for y in range(4):
            for z in range(4):
                for c in range(2):
                    pairs.append((flat(x, y, z, c), flat(*move(x, y, z, c))))
    return sorted(pairs)


def turn(c):
    return 1 - 2 * c


XF = table(lambda x, y, z, c: (x + turn(c), y, z, c))
XG = table(lambda x, y, z, c: (x - turn(c), y, z, c))
YF = table(lambda x, y, z, c: (x, y + turn(c), z, c))
YG = table(lambda x, y, z, c: (x, y - turn(c), z, c))
ZF = table(lambda x, y, z, c: (x, y, z + turn(c), c))
ZG = table(lambda x, y, z, c: (x, y, z - turn(c), c))
Y2 = table(lambda x, y, z, c: (x, y + 2, z, c))
Z2 = table(lambda x, y, z, c: (x, y, z + 2, c))
ZN = table(lambda x, y, z, c: (x, y, z ^ 1, c))
CC = table(lambda x, y, z, c: (x, y, z, 1 - c))
ZNC = table(lambda x, y, z, c: (x, y, z ^ 1, 1 - c))


def send(v, pairs):
    return lax.ppermute(v, AXES, pairs)


def call(kernel, outs, out_specs, in_specs, scratch, flops=0, aliases=None, limit=16):
    return pl.pallas_call(
        kernel,
        out_shape=outs,
        in_specs=in_specs,
        out_specs=out_specs,
        scratch_shapes=scratch,
        input_output_aliases=aliases or {},
        compiler_params=pltpu.CompilerParams(vmem_limit_bytes=limit << 20),
        cost_estimate=pl.CostEstimate(flops=flops, bytes_accessed=4 << 20, transcendentals=0),
    )


def sems(*shape):
    return pltpu.SemaphoreType.DMA(shape)


def run_copies(copies):
    for copy in copies:
        copy.start()
    return copies


def finish_copies(copies):
    for copy in copies:
        copy.wait()


def first_kernel(slots, idx, *refs):
    n = len(slots)
    ws, bs, outs, (wv, bv, ov, wsem, bsem, osem) = refs[:16], refs[16:20], refs[20 : 20 + n], refs[20 + n :]

    def w_copy(at, q, k):
        place = wv.at[at, pl.ds(q // 2 * 256, 256), pl.ds(q % 2 * 1024, 1024)]
        return pltpu.make_async_copy(ws[q * 4 + k], place, wsem.at[at, q])

    def b_place(v):
        return bv.at[v % 2, pl.ds(pl.multiple_of(v // 2 * 1024, 1024), 1024)]

    b_copies = run_copies([pltpu.make_async_copy(bs[k], b_place(idx[4 + k]), bsem.at[k]) for k in range(4)])
    for at, j in enumerate(slots):
        for k in range(4):

            @pl.when(idx[j] == k)
            def _(at=at, k=k):
                run_copies([w_copy(at, q, k) for q in range(4)])

    finish_copies(b_copies)
    writes = []
    for at in range(n):
        finish_copies([w_copy(at, q, 0) for q in range(4)])
        for low in range(2):
            acc = jnp.dot(wv[at], bv[low], preferred_element_type=F32)
            ov[at, :, low * 256 : (low + 1) * 256] = acc.astype(BF)
        writes += run_copies([pltpu.make_async_copy(ov.at[at], outs[at], osem.at[at])])
    finish_copies(writes)


def first_product(slots, idx, ws, bs):
    n = len(slots)
    scratch = [
        pltpu.VMEM((n, 512, 2048), BF),
        pltpu.VMEM((2, 2048, 256), BF),
        pltpu.VMEM((n, 512, 512), BF),
        sems(n, 4),
        sems(4),
        sems(n),
    ]
    return call(
        functools.partial(first_kernel, slots),
        ((pltpu.HBM if n == 4 else jax.ShapeDtypeStruct)((512, 512), BF),) * n,
        (HBM if n == 4 else ANY,) * n,
        [SMEM] + [ANY] * 20,
        scratch,
        flops=n * 2 * 512 * 2048 * 512,
        limit=3 + (5 * n + 1) // 2,
    )(idx, *ws, *bs)


def split_kernel(idx, a, b, c, o0, o1, o2, o3):
    for k, out in enumerate((o0, o1, o2, o3)):
        at = pl.ds(pl.multiple_of(idx[k] * 128, 128), 128)
        total = a[:, at].astype(F32) + b[:, at].astype(F32) + c[:, at].astype(F32)
        out[...] = total.astype(BF)


def split_sum(idx, a, b, c):
    out = jax.ShapeDtypeStruct((a.shape[0], 128), BF)
    return pl.pallas_call(
        split_kernel,
        out_shape=(out,) * 4,
        in_specs=[SMEM] + [VMEM] * 3,
        out_specs=(VMEM,) * 4,
        compiler_params=pltpu.CompilerParams(vmem_limit_bytes=8 << 20),
        cost_estimate=pl.CostEstimate(flops=3 * a.size, bytes_accessed=8 * a.size, transcendentals=0),
        name="split_sum",
    )(idx, a, b, c)


def load_b_kernel(idx, *refs):
    bs, bv, sem = refs[:16], refs[16], refs[17]
    copies = []
    for i in range(2):
        for k in range(8):
            v = idx[k]
            at = pl.ds(pl.multiple_of(i * 2048 + v // 4 * 1024, 1024), 1024)
            copies.append(pltpu.make_async_copy(bs[i * 8 + k], bv.at[v % 4, at], sem.at[i * 8 + k]))
    finish_copies(run_copies(copies))


def load_b(idx, bs):
    return call(
        load_b_kernel,
        jax.ShapeDtypeStruct((4, 4096, 256), BF),
        VMEM,
        [SMEM] + [ANY] * 16,
        [sems(16)],
        limit=1,
    )(idx, *bs)


def second_kernel(ks, idx, bv, *refs):
    n_ts = len(ks) * len(CHUNKS)
    ts, refs = refs[:n_ts], refs[n_ts:]
    last = ks == (2,)
    if last:
        own, near, outs, refs = refs[0], refs[1], refs[2:6], refs[6:]
        every, esem, osem = refs[:3]
        refs = refs[3:]
        moves = run_copies(
            [
                pltpu.make_async_copy(own, every.at[0], esem.at[0]),
                pltpu.make_async_copy(near.at[pl.ds(0, 128)], every.at[1], esem.at[1]),
                pltpu.make_async_copy(near.at[pl.ds(128, 128)], every.at[3], esem.at[2]),
            ]
        )
    else:
        out, refs = refs[0], refs[1:]
    tt, tsem, tvs = refs[0], refs[1], refs[2:]
    copies = []
    for q, blocks in enumerate(CHUNKS):
        for n in range(len(ks)):
            m = q * len(ks) + n
            copies.append((q, n, pltpu.make_async_copy(ts[m], tvs[q].at[n], tsem.at[m])))
    run_copies([copy for _, _, copy in copies])
    for q, n, copy in copies:
        copy.wait()
        for rz in range(4):
            for r, (ch, i) in enumerate(CHUNKS[q]):
                at = pl.ds(pl.multiple_of(i * 2048 + idx[8 + rz * 2 + ch] * 256, 256), 256)
                tt[n * 128 : (n + 1) * 128, at] = tvs[q][n, rz, r * 256 : (r + 1) * 256, :].T
    for n in range(4):
        at = slice(n * 256, (n + 1) * 256)
        acc = jnp.dot(tt[...], bv[n], preferred_element_type=F32).astype(BF)
        if last:
            every[2, :, at] = acc
        else:
            out[:, at] = acc
    if last:
        finish_copies(moves)
        finish_copies(
            run_copies([pltpu.make_async_copy(every.at[idx[16 + j]], outs[j], osem.at[j]) for j in range(4)])
        )


def second_product(ks, idx, bv, ts, *early):
    n = len(ks)
    scratch = [pltpu.VMEM((n * 128, 4096), BF), sems(n * len(CHUNKS))]
    scratch += [pltpu.VMEM((n, 4, 256 * len(blocks), 128), BF) for blocks in CHUNKS]
    if early:
        outs, specs = (jax.ShapeDtypeStruct((128, 1024), BF),) * 4, (ANY,) * 4
        scratch = [pltpu.VMEM((4, 128, 1024), BF), sems(3), sems(4)] + scratch
    else:
        outs, specs = jax.ShapeDtypeStruct((n * 128, 1024), BF), VMEM
    return call(
        functools.partial(second_kernel, ks),
        outs,
        specs,
        [SMEM, VMEM] + [ANY] * (n * len(CHUNKS) + len(early)),
        scratch,
        flops=2 * n * 128 * 4096 * 1024,
        limit=12,
    )(idx, bv, *ts, *early)


def tail_kernel(idx, a, b, c, d, o0, o1, o2, o3):
    for k, out in enumerate((o0, o1, o2, o3)):
        at = pl.ds(pl.multiple_of(idx[k] * 256, 256), 256)
        total = a[:, at].astype(F32) + b[:, at].astype(F32)
        total += c[:, at].astype(F32) + d[:, at].astype(F32)
        out[...] = total.astype(out.dtype)


def tail_split(idx, a, b, c, d):
    rows = a.shape[0]
    near = jax.ShapeDtypeStruct((rows, 256), BF)
    return pl.pallas_call(
        tail_kernel,
        out_shape=(jax.ShapeDtypeStruct((rows, 256), F32), near, near, near),
        in_specs=[SMEM] + [VMEM] * 4,
        out_specs=(VMEM,) * 4,
        compiler_params=pltpu.CompilerParams(vmem_limit_bytes=8 << 20),
        name="tail_split",
    )(idx, a, b, c, d)


def finish_kernel(idx, density, p0, p1, p2, p3, out):
    for k, piece in enumerate((p0, p1, p2, p3)):
        at = pl.ds(pl.multiple_of(idx[k] * 128, 128), 128)
        out[at, :] = density[at, :] + piece[...].astype(F32)


def finish(idx, density, pieces):
    return pl.pallas_call(
        finish_kernel,
        out_shape=jax.ShapeDtypeStruct(density.shape, F32),
        in_specs=[SMEM] + [VMEM] * 5,
        out_specs=VMEM,
        compiler_params=pltpu.CompilerParams(vmem_limit_bytes=8 << 20),
        name="finish",
    )(idx, density, *pieces)


def ints(values):
    return jnp.stack([jnp.asarray(v, jnp.int32) for v in values])


def step(orbitals, screened, density_in):
    zh, y, zl, x, c = (lax.axis_index(name) for name in AXES)
    z = 2 * zh + zl
    s = 1 - 2 * c
    mod4 = lambda v: lax.rem(v + 8, 4)
    z_at = [mod4(z + s * k) for k in range(4)]
    piece = [mod4(j - s * (x - y)) for j in range(4)]
    first_idx = ints(piece + [(v // 2 ^ zh) * 2 + v % 2 for v in z_at])
    split_idx = ints([z, mod4(z + s), mod4(z - s), mod4(z + 2)])
    from_z = [z, mod4(z - s), mod4(z + s), mod4(z + 2)]
    places = [((v % 2) * 2 + core) * 2 + v // 2 for v in from_z for core in (c, 1 - c)]
    b2_slot = [(v // 2) * 4 + (v % 2) * 2 + core for core in (c, 1 - c) for v in z_at]
    second_idx = ints(b2_slot + places + piece)
    tail_idx = ints([zl * 2 + c, (1 - zl) * 2 + c, zl * 2 + 1 - c, (1 - zl) * 2 + 1 - c])
    finish_idx = ints([c * 2 + zl, c * 2 + 1 - zl, (1 - c) * 2 + zl, (1 - c) * 2 + 1 - zl])

    keep = lax.dynamic_slice_in_dim(screened, zh * 256, 256, 0)
    give = lax.dynamic_slice_in_dim(screened, (1 - zh) * 256, 256, 0)
    b = jnp.transpose(orbitals, (1, 0, 2))
    b0, b1 = b[0], b[1]
    other = send(give, Z2)
    wa_f = send(keep, XF)
    wa_g = send(keep, XG)
    b0_f = send(b0, ZF)
    b0_g = send(b0, ZG)
    wa_ff = send(wa_g, XG)
    wb_f = send(other, XF)
    wb_g = send(other, XG)
    b0_ff = send(b0_g, ZG)
    b1_f = send(b1, ZF)
    b1_g = send(b1, ZG)
    wb_ff = send(wb_f, XF)
    b1_ff = send(b1_f, ZF)
    wa = (keep, wa_g, wa_ff, wa_f)
    wb = (other, wb_g, wb_ff, wb_f)
    swap = lambda four: tuple(send(four[k], CC) for k in (0, 3, 2, 1))
    ws = wa + wb + swap(wa) + swap(wb)
    bs = ((b0, b0_g, b0_ff, b0_f), (b1, b1_g, b1_ff, b1_f))

    t2, t1, t3, t0 = [None] * 2, [None] * 2, [None] * 2, [None] * 2
    (t2[0],) = first_product((2,), first_idx, ws, bs[0])
    t1[0], t3[0], t0[0] = first_product((1, 3, 0), first_idx, ws, bs[0])
    t2[1], t1[1], t3[1], t0[1] = first_product((2, 1, 3, 0), first_idx, ws, bs[1])
    gathered = []
    for i in range(2):
        r1 = send(t2[i], YF)
        mid = (t1[i].astype(F32) + r1.astype(F32)).astype(BF)
        r_g = send(t3[i], YG)
        r_f = send(mid, YF)
        t_own, t_f, t_g, t_2 = split_sum(split_idx, t0[i], r_f, r_g)
        t_2 = send(t_2, Z2)
        t_f = send(t_f, ZF)
        t_g = send(t_g, ZG)
        four = [t_own, t_f, t_g, t_2]
        halves = [four] if i == 0 else [[t[:256] for t in four], [t[256:] for t in four]]
        for t in halves:
            n = len(gathered)
            t = jnp.stack(t)
            f = send(t, XF)
            g = send(t, XG)
            far = send(g, XG) if n else send(f, XF)
            gathered.append((t, g, far, f))
    b_all = load_b(second_idx, [v for i in range(2) for v in bs[i] + swap(bs[i])])

    def second(ks, *more):
        return second_product(ks, second_idx, b_all, [t[k] for t in gathered for k in ks], *more)

    own, near = second((0,)), second((1, 3))
    d0, d1, d2, d3 = second((2,), own, near)

    d2, d1, d3 = send(d2, Y2), send(d1, YF), send(d3, YG)
    p_own, p_n, p_c, p_nc = tail_split(tail_idx, d0, d1, d3, d2)
    p_nc = send(p_nc, ZNC)
    p_n = send(p_n, ZN)
    p_c = send(p_c, CC)
    return finish(finish_idx, density_in, (p_own, p_n, p_c, p_nc))


def solution(mesh):
    fine = Mesh(mesh.devices.reshape(2, 4, 2, 4, 2), AXES)
    row, col = ("zh", "y"), ("zl", "x", "c")
    return jax.shard_map(
        step,
        mesh=fine,
        in_specs=(P(row, None, col), P(col, row), P(row, col)),
        out_specs=P(row, col),
        check_vma=False,
    )
```
